32 devices in a mesh: rep: 4 (over x, core), shard: 8 (over z, y).
Axes of the slice: x: 2, y: 2, z: 4, core: 2. Of those that a mesh axis runs over, the one named last changes fastest.
Arguments:
- tokens: bfloat16 [32, 1024, 768], P(('rep', 'shard')), may hold values from -6 to 6
- cotangent: bfloat16 [32, 1024, 768], P(('rep', 'shard')), may hold values from -6 to 6
- segments: int32 [32, 1024], P(('rep', 'shard')), may hold values from -1 to 7, as said below
- first_pos: int32 [32, 8], P(('rep', 'shard')), may hold values from 0 to 959, as said below
- labels: int32 [32, 8], P(('rep', 'shard')), may hold values from 0 to 2
- query_weight: bfloat16 [768, 768], P('shard'), may hold values from -0.21875 to 0.21875
- key_weight: bfloat16 [768, 768], P('shard'), may hold values from -0.21875 to 0.21875
- value_weight: bfloat16 [768, 768], P('shard'), may hold values from -0.21875 to 0.21875
- out_weight: bfloat16 [768, 768], P('shard'), may hold values from -0.875 to 0.875
- up_weight: bfloat16 [768, 3072], P('shard'), may hold values from -0.21875 to 0.21875
- down_weight: bfloat16 [3072, 768], P('shard'), may hold values from -0.109375 to 0.109375
- pool_weight: bfloat16 [768, 768], P('shard'), may hold values from -0.21875 to 0.21875
- class_weight: bfloat16 [768, 3], P('shard'), may hold values from -0.21875 to 0.21875
- query_bias: bfloat16 [768], P('shard'), may hold values from -3 to 3
- value_bias: bfloat16 [768], P('shard'), may hold values from -3 to 3
- out_bias: bfloat16 [768], P('shard'), may hold values from -3 to 3
- norm1_gain: bfloat16 [768], P('shard'), may hold values from 0.5 to 1.5
- norm1_shift: bfloat16 [768], P('shard'), may hold values from -3 to 3
- up_bias: bfloat16 [3072], P('shard'), may hold values from -3 to 3
- down_bias: bfloat16 [768], P('shard'), may hold values from -3 to 3
- norm2_gain: bfloat16 [768], P('shard'), may hold values from 0.5 to 1.5
- norm2_shift: bfloat16 [768], P('shard'), may hold values from -3 to 3
- pool_bias: bfloat16 [768], P('shard'), may hold values from -3 to 3
- class_bias: bfloat16 [3], replicated, may hold values from -3 to 3
Outputs:
- output: bfloat16 [32, 1024, 768], P(('rep', 'shard'))
- logits: float32 [32, 8, 3], P(('rep', 'shard'))
- input_grad: float32 [32, 1024, 768], P(('rep', 'shard'))
- query_weight_grad: float32 [768, 768], P('shard')
- key_weight_grad: float32 [768, 768], P('shard')
- value_weight_grad: float32 [768, 768], P('shard')
- out_weight_grad: float32 [768, 768], P('shard')
- up_weight_grad: float32 [768, 3072], P('shard')
- down_weight_grad: float32 [3072, 768], P('shard')
- pool_weight_grad: float32 [768, 768], P('shard')
- class_weight_grad: float32 [768, 3], P('shard')
- query_bias_grad: float32 [768], P('shard')
- value_bias_grad: float32 [768], P('shard')
- out_bias_grad: float32 [768], P('shard')
- norm1_gain_grad: float32 [768], P('shard')
- norm1_shift_grad: float32 [768], P('shard')
- up_bias_grad: float32 [3072], P('shard')
- down_bias_grad: float32 [768], P('shard')
- norm2_gain_grad: float32 [768], P('shard')
- norm2_shift_grad: float32 [768], P('shard')
- pool_bias_grad: float32 [768], P('shard')
- class_bias_grad: float32 [3], replicated
- rms: float32 [4], replicated
The draws below stay inside these ranges and needn't reach their ends.
Inputs may be any that keep to these rules, and one draw needn't show every extreme that they name: `segments`: in each sequence the tokens of documents 0 to 7 come in order, each document one or more tokens, followed by one or more padding tokens numbered -1; document lengths are heavy-tailed. `first_pos`: the first position of each document, consistent with segments, rising within a sequence; the first document starts at 0.
All inputs are finite; a program needn't handle non-finite values.
Results may differ from the reference program's by a relative error of at most 0.017.
Values may be sent and summed in bfloat16 or wider, within the bound.
No kernel may reach another device: no remote copies, remote signals or barrier semaphores. Data moves between devices by JAX's collectives and lax.ppermute only.
A program may use at most 256 MiB of HBM per device.

```python
import math
import jax
import jax.numpy as jnp
from jax import lax

D = 768
HEADS = 12
HEAD_DIM = 64
FF = 3072
CLS = 3
DOCS = 8
LEN = 1024
SEQS = 32


def doc_starts(key):
    base = jax.random.fold_in(key, 7)
    pad_key, weight_key = jax.random.split(base)
    padding = jax.random.randint(pad_key, (SEQS, 1), max(LEN // 16, 1), 2 * LEN // 3 + 1)
    real_len = LEN - padding
    draws_int = jax.random.randint(weight_key, (SEQS, DOCS), 1, 17)
    weights_int = draws_int * draws_int * draws_int
    weight_total = jnp.sum(weights_int, axis=1, keepdims=True)
    doc_lengths = 1 + (real_len - DOCS) * weights_int // weight_total
    last_len = real_len[:, 0] - jnp.sum(doc_lengths[:, :-1], axis=1)
    doc_lengths = jnp.concatenate([doc_lengths[:, :-1], last_len[:, None]], axis=1)
    starts = jnp.cumsum(doc_lengths, axis=1) - doc_lengths
    return (starts.astype(jnp.int32), real_len.astype(jnp.int32))


def draw_first_pos(key, part):
    return doc_starts(key)[0]


def draw_segments(key, part):
    starts, real_len = doc_starts(key)
    positions = jnp.arange(LEN, dtype=jnp.int32)
    inside = positions[None, :, None] >= starts[:, None, :]
    segment = jnp.sum(inside.astype(jnp.int32), axis=2) - 1
    return jnp.where(positions[None, :] < real_len, segment, -1).astype(jnp.int32)


def place_ends(values, key, smallest, top_value):
    shape = values.shape
    spot = [jax.random.randint(jax.random.fold_in(key, axis), (), 0, shape[axis]) for axis in range(len(shape))]
    values = values.at[tuple(spot)].set(smallest)
    longest = shape.index(max(shape))
    spot[longest] = (spot[longest] + 1) % shape[longest]
    return values.at[tuple(spot)].set(top_value)


def block_scale(key, dims, cuts, least, top_value):
    level = 1.0
    for dim, parts in cuts:
        draws = jax.random.uniform(jax.random.fold_in(jax.random.fold_in(key, 6), dim), (parts,), jnp.float32, least / len(cuts), top_value / len(cuts))
        level = level * jnp.repeat(jnp.exp(draws), dims[dim] // parts).reshape((-1,) + (1,) * (len(dims) - 1 - dim))
    return level


def scatter_about(stream_key, extent, scale, reach, shards=(), kind=jnp.bfloat16):
    factor_of = block_scale(stream_key, extent, shards, -0.22, 0.18) if shards else 1.0
    result = jax.random.normal(stream_key, extent, jnp.float32) * scale * factor_of
    return jnp.minimum(jnp.maximum(result, -reach), reach).astype(kind)


def setup_inputs(seed: int = 0) -> dict:
    key_list = jax.random.split(jax.random.key(seed), 25)
    tokens = scatter_about(key_list[0], (SEQS, LEN, D), 1.0, 6.0, ((0, 32),))
    cotangent = scatter_about(key_list[1], (SEQS, LEN, D), 1.0, 6.0, ((0, 32),))
    segments = draw_segments(jax.random.fold_in(key_list[24], 71), 0)
    first_pos = draw_first_pos(jax.random.fold_in(key_list[24], 71), 0)
    labels = place_ends(jax.random.randint(key_list[4], (SEQS, DOCS), 0, CLS), jax.random.fold_in(key_list[4], 1), 0, CLS - 1).astype(jnp.int32)
    query_weight = scatter_about(key_list[5], (D, D), D ** -0.5, 0.21875, ((0, 8),))
    key_weight = scatter_about(key_list[6], (D, D), D ** -0.5, 0.21875, ((0, 8),))
    value_weight = scatter_about(key_list[7], (D, D), D ** -0.5, 0.21875, ((0, 8),))
    out_weight = scatter_about(key_list[8], (D, D), (D // 16) ** -0.5, 0.875, ((0, 8),))
    up_weight = scatter_about(key_list[9], (D, FF), D ** -0.5, 0.21875, ((0, 8),))
    down_weight = scatter_about(key_list[10], (FF, D), FF ** -0.5, 0.109375, ((0, 8),))
    pool_weight = scatter_about(key_list[11], (D, D), D ** -0.5, 0.21875, ((0, 8),))
    class_weight = scatter_about(key_list[12], (D, CLS), D ** -0.5, 0.21875, ((0, 8),))
    query_bias = scatter_about(key_list[13], (D,), 0.5, 3.0, ((0, 8),))
    value_bias = scatter_about(key_list[14], (D,), 0.5, 3.0, ((0, 8),))
    out_bias = scatter_about(key_list[15], (D,), 0.5, 3.0, ((0, 8),))
    norm1_gain = jnp.clip(1.0 + 0.1 * jax.random.normal(key_list[16], (D,), jnp.float32), 0.5, 1.5).astype(jnp.bfloat16)
    norm1_shift = scatter_about(key_list[17], (D,), 0.5, 3.0, ((0, 8),))
    up_bias = scatter_about(key_list[18], (FF,), 0.5, 3.0, ((0, 8),))
    down_bias = scatter_about(key_list[19], (D,), 0.5, 3.0, ((0, 8),))
    norm2_gain = jnp.clip(1.0 + 0.1 * jax.random.normal(key_list[20], (D,), jnp.float32), 0.5, 1.5).astype(jnp.bfloat16)
    norm2_shift = scatter_about(key_list[21], (D,), 0.5, 3.0, ((0, 8),))
    pool_bias = scatter_about(key_list[22], (D,), 0.5, 3.0, ((0, 8),))
    class_bias = scatter_about(key_list[23], (CLS,), 1.0, 3.0)
    return {"tokens": tokens, "cotangent": cotangent, "segments": segments, "first_pos": first_pos, "labels": labels, "query_weight": query_weight, "key_weight": key_weight, "value_weight": value_weight, "out_weight": out_weight, "up_weight": up_weight, "down_weight": down_weight, "pool_weight": pool_weight, "class_weight": class_weight, "query_bias": query_bias, "value_bias": value_bias, "out_bias": out_bias, "norm1_gain": norm1_gain, "norm1_shift": norm1_shift, "up_bias": up_bias, "down_bias": down_bias, "norm2_gain": norm2_gain, "norm2_shift": norm2_shift, "pool_bias": pool_bias, "class_bias": class_bias}


@jax.custom_vjp
def low(v):
    return lax.optimization_barrier(v.astype(jnp.bfloat16)).astype(jnp.float32)

@jax.custom_vjp
def low_back(v):
    return v

def low_keep(v):
    return (low(v), None)

def low_pass(kept, grad):
    return (grad,)

def back_keep(v):
    return (v, None)

def back_low(kept, grad):
    return (low(grad),)
low.defvjp(low_keep, low_pass)
low_back.defvjp(back_keep, back_low)
highest = lax.Precision.HIGHEST
epsilon = 1e-12

def rounded_both(value):
    return low_back(low(value))

def matmul(left, right):
    return jnp.dot(left, right, precision=highest)

def layer_norm(value, gain, shift):
    mean_val = lax.optimization_barrier(jnp.mean(value, axis=-1, keepdims=True))
    centred = value - mean_val
    variance = lax.optimization_barrier(jnp.mean(centred * centred, axis=-1, keepdims=True))
    return centred * lax.rsqrt(variance + epsilon) * gain + shift

def attend_one(inputs):
    query_rows, key_rows, value_rows, segment = inputs
    length = query_rows.shape[0]
    query_heads = query_rows.reshape(length, HEADS, HEAD_DIM)
    key_heads = key_rows.reshape(length, HEADS, HEAD_DIM)
    value_heads = value_rows.reshape(length, HEADS, HEAD_DIM)
    scaling = 1.0 / math.sqrt(HEAD_DIM)
    scores = low_back(jnp.einsum('qhe,khe->hqk', query_heads, key_heads, precision=highest) * scaling)
    allowed = (segment[:, None] == segment[None, :])[None]
    masked = jnp.where(allowed, scores, -1e+30)
    row_peak = lax.optimization_barrier(jnp.max(masked, axis=-1, keepdims=True))
    expo = jnp.exp(masked - row_peak)
    probs = low(expo / lax.optimization_barrier(jnp.sum(expo, axis=-1, keepdims=True)))
    context = jnp.einsum('hqk,khe->qhe', probs, value_heads, precision=highest)
    return context.reshape(length, HEADS * HEAD_DIM)

def forward(params, tokens, segments, first_pos, labels):
    query_weight, key_weight, value_weight, out_weight, up_weight, down_weight, pool_weight, class_weight, query_bias, value_bias, out_bias, norm1_gain, norm1_shift, up_bias, down_bias, norm2_gain, norm2_shift, pool_bias, class_bias = params
    group_size, length, width = tokens.shape
    flat_rows = tokens.reshape(group_size * length, width)
    tokens_low = low(flat_rows)
    queries = rounded_both(matmul(tokens_low, query_weight) + query_bias)
    key_rows = rounded_both(matmul(tokens_low, key_weight))
    value_rows = rounded_both(matmul(tokens_low, value_weight) + value_bias)
    context = lax.map(jax.checkpoint(attend_one), (queries.reshape(group_size, length, width), key_rows.reshape(group_size, length, width), value_rows.reshape(group_size, length, width), segments))
    context = rounded_both(context.reshape(group_size * length, width))
    attended = low_back(matmul(context, out_weight) + out_bias)
    first_sum = flat_rows + attended
    normed = layer_norm(first_sum, norm1_gain, norm1_shift)
    pre_act = low_back(matmul(low(normed), up_weight) + up_bias)
    hidden = low(jax.nn.gelu(pre_act, approximate=False))
    ffn_out = low_back(matmul(hidden, down_weight) + down_bias)
    second_sum = normed + ffn_out
    output_f = layer_norm(second_sum, norm2_gain, norm2_shift)
    output_seq = output_f.reshape(group_size, length, width)
    heads_rows = jnp.take_along_axis(output_seq, first_pos[:, :, None], axis=1)
    picked = low(heads_rows.reshape(-1, width))
    pool_pre = low_back(matmul(picked, pool_weight) + pool_bias)
    pooled = low(jnp.tanh(pool_pre))
    logits = matmul(pooled, class_weight) + class_bias
    class_peak = lax.optimization_barrier(jnp.max(logits, axis=-1, keepdims=True))
    log_total = class_peak[:, 0] + jnp.log(lax.optimization_barrier(jnp.sum(jnp.exp(logits - class_peak), axis=-1)))
    targets = (labels.reshape(-1)[:, None] == jnp.arange(CLS, dtype=jnp.int32)[None, :]).astype(jnp.float32)
    loss = jnp.sum(log_total - lax.optimization_barrier(jnp.sum(logits * targets, axis=-1)))
    valid = (segments.reshape(-1) >= 0).astype(jnp.float32)
    sums = jnp.stack([jnp.sum(valid * lax.optimization_barrier(jnp.sum(first_sum * first_sum, axis=-1))), jnp.sum(valid * lax.optimization_barrier(jnp.sum(attended * attended, axis=-1))), jnp.sum(valid * lax.optimization_barrier(jnp.sum(second_sum * second_sum, axis=-1))), jnp.sum(valid * lax.optimization_barrier(jnp.sum(ffn_out * ffn_out, axis=-1)))])
    return ((output_seq, logits.reshape(group_size, DOCS, CLS), loss), (sums, jnp.sum(valid)))

def reference(tokens, cotangent, segments, first_pos, labels, query_weight, key_weight, value_weight, out_weight, up_weight, down_weight, pool_weight, class_weight, query_bias, value_bias, out_bias, norm1_gain, norm1_shift, up_bias, down_bias, norm2_gain, norm2_shift, pool_bias, class_bias):
    params = tuple((item.astype(jnp.float32) for item in (query_weight, key_weight, value_weight, out_weight, up_weight, down_weight, pool_weight, class_weight, query_bias, value_bias, out_bias, norm1_gain, norm1_shift, up_bias, down_bias, norm2_gain, norm2_shift, pool_bias, class_bias)))
    group_size = math.gcd(SEQS, max(1, 4096 // LEN))
    step_count = SEQS // group_size

    def blocked(values_in):
        return values_in.reshape((step_count, group_size) + values_in.shape[1:])

    def one_step(running, inputs):
        grad_sum, stat_sum, valid_sum = running
        token_block, cot_block, seg_block, first_block, label_block = inputs

        def wrapped(param_list, token_f32):
            return forward(param_list, token_f32, seg_block, first_block, label_block)
        primal, pullback, extras = jax.vjp(wrapped, params, token_block.astype(jnp.float32), has_aux=True)
        grad_params, grad_tokens = pullback((cot_block.astype(jnp.float32), jnp.zeros_like(primal[1]), jnp.ones_like(primal[2])))
        grad_sum = jax.tree.map(lambda left, right: left + right, grad_sum, grad_params)
        return ((grad_sum, stat_sum + extras[0], valid_sum + extras[1]), (primal[0].astype(jnp.bfloat16), primal[1], grad_tokens))
    start = (tuple((jnp.zeros_like(item) for item in params)), jnp.zeros((4,), jnp.float32), jnp.zeros((), jnp.float32))
    finals, outputs = lax.scan(one_step, start, (blocked(tokens), blocked(cotangent), blocked(segments), blocked(first_pos), blocked(labels)))
    grads, stat_sum, valid_sum = finals
    output = outputs[0].reshape(SEQS, LEN, D)
    logits = outputs[1].reshape(SEQS, DOCS, CLS)
    input_grad = outputs[2].reshape(SEQS, LEN, D)
    rms = jnp.sqrt(stat_sum / (valid_sum * D))
    return (output, logits, input_grad, grads[0], grads[1], grads[2], grads[3], grads[4], grads[5], grads[6], grads[7], grads[8], grads[9], grads[10], grads[11], grads[12], grads[13], grads[14], grads[15], grads[16], grads[17], grads[18], rms)
```

```python
from functools import partial
import math

import jax
import jax.numpy as jnp
from jax import lax
from jax.sharding import PartitionSpec as P

epsilon = 1e-12
highest = lax.Precision.HIGHEST


def product(left, right):
    return jnp.dot(left, right, preferred_element_type=jnp.float32)


def product_left(left, right):
    return lax.dot_general(
        left, right, (((0,), (0,)), ((), ())), preferred_element_type=jnp.float32
    )


def product_right(left, right):
    return lax.dot_general(
        left, right, (((1,), (1,)), ((), ())), preferred_element_type=jnp.float32
    )


def norm_forward(value, gain, shift):
    mean_val = jnp.mean(value, axis=-1, keepdims=True)
    centred = value - mean_val
    variance = jnp.mean(centred * centred, axis=-1, keepdims=True)
    inverse = lax.rsqrt(variance + epsilon)
    normal = centred * inverse
    return (normal * gain + shift, normal, inverse)


def norm_backward(grad_out, normal, inverse, gain):
    scaled = grad_out * gain
    grad_in = inverse * (
        scaled
        - jnp.mean(scaled, axis=-1, keepdims=True)
        - normal * jnp.mean(scaled * normal, axis=-1, keepdims=True)
    )
    return (grad_in, jnp.sum(grad_out * normal, axis=0), jnp.sum(grad_out, axis=0))


def block_inputs(
    queries, key_seqs, value_seqs, segments, block_id, block_rows, blocks_per, head_count
):
    seq_count, length, model_width = queries.shape
    head_size = model_width // head_count
    seq_id = block_id // blocks_per
    row_start = block_id % blocks_per * block_rows
    query_block = lax.dynamic_slice(queries, (seq_id, row_start, 0), (1, block_rows, model_width))[
        0
    ]
    key_seq = lax.dynamic_index_in_dim(key_seqs, seq_id, 0, False).reshape(
        length, head_count, head_size
    )
    value_seq = lax.dynamic_index_in_dim(value_seqs, seq_id, 0, False).reshape(
        length, head_count, head_size
    )
    seg_seq = lax.dynamic_index_in_dim(segments, seq_id, 0, False)
    seg_query = lax.dynamic_slice_in_dim(seg_seq, row_start, block_rows)
    scaling = 1.0 / math.sqrt(head_size)
    query_heads = query_block.reshape(block_rows, head_count, head_size)
    scores = (
        jnp.einsum("qhe,khe->hqk", query_heads, key_seq, preferred_element_type=jnp.float32)
        * scaling
    )
    allowed = (seg_query[:, None] == seg_seq[None, :])[None]
    masked = jnp.where(allowed, scores, -1e30)
    return (seq_id, row_start, query_heads, key_seq, value_seq, masked, scaling)


def attention_forward(queries, key_seqs, value_seqs, segments, head_count):
    seq_count, length, model_width = queries.shape
    block_rows = min(512, length)
    blocks_per = length // block_rows

    def one_block(block_id):
        parts_in = block_inputs(
            queries, key_seqs, value_seqs, segments, block_id, block_rows, blocks_per, head_count
        )
        masked = parts_in[5]
        value_seq = parts_in[4]
        row_peak = jnp.max(masked, axis=-1, keepdims=True)
        expo = jnp.exp(masked - row_peak)
        row_total = jnp.sum(expo, axis=-1, keepdims=True)
        weights_low = (expo / row_total).astype(jnp.bfloat16)
        context = jnp.einsum(
            "hqk,khe->qhe", weights_low, value_seq, preferred_element_type=jnp.float32
        )
        return (
            context.reshape(block_rows, model_width).astype(jnp.bfloat16),
            row_peak[..., 0] + jnp.log(row_total[..., 0]),
        )

    block_ids = jnp.arange(seq_count * blocks_per, dtype=jnp.int32)
    context, logsum = lax.map(one_block, block_ids)
    return (context.reshape(seq_count, length, model_width), logsum)


def attention_backward(queries, key_seqs, value_seqs, segments, logsum, grad_context, head_count):
    seq_count, length, model_width = queries.shape
    block_rows = min(512, length)
    blocks_per = length // block_rows
    head_size = model_width // head_count

    def one_block(block_id):
        seq_id, row_start, query_heads, key_seq, value_seq, masked, scaling = block_inputs(
            queries, key_seqs, value_seqs, segments, block_id, block_rows, blocks_per, head_count
        )
        grad_block = lax.dynamic_slice(
            grad_context, (seq_id, row_start, 0), (1, block_rows, model_width)
        )[0]
        grad_heads = grad_block.reshape(block_rows, head_count, head_size)
        logsum_block = lax.dynamic_index_in_dim(logsum, block_id, 0, False)
        probs = jnp.exp(masked - logsum_block[..., None])
        grad_probs = jnp.einsum(
            "qhe,khe->hqk", grad_heads, value_seq, preferred_element_type=jnp.float32
        )
        inner = jnp.sum(grad_probs * probs, axis=-1, keepdims=True)
        grad_scores = (probs * (grad_probs - inner)).astype(jnp.bfloat16)
        grad_query = (
            jnp.einsum("hqk,khe->qhe", grad_scores, key_seq, preferred_element_type=jnp.float32)
            * scaling
        )
        grad_key = (
            jnp.einsum("hqk,qhe->khe", grad_scores, query_heads, preferred_element_type=jnp.float32)
            * scaling
        )
        grad_value = jnp.einsum(
            "hqk,qhe->khe",
            probs.astype(jnp.bfloat16),
            grad_heads,
            preferred_element_type=jnp.float32,
        )
        return (
            grad_query.reshape(block_rows, model_width),
            grad_key.reshape(length, model_width),
            grad_value.reshape(length, model_width),
        )

    block_ids = jnp.arange(seq_count * blocks_per, dtype=jnp.int32)
    grad_query, grad_key, grad_value = lax.map(one_block, block_ids)
    grad_query = grad_query.reshape(seq_count * length, model_width).astype(jnp.bfloat16)
    grad_key = jnp.sum(grad_key.reshape(seq_count, blocks_per, length, model_width), axis=1)
    grad_value = jnp.sum(grad_value.reshape(seq_count, blocks_per, length, model_width), axis=1)
    grad_key = grad_key.reshape(seq_count * length, model_width).astype(jnp.bfloat16)
    grad_value = grad_value.reshape(seq_count * length, model_width).astype(jnp.bfloat16)
    return (grad_query, grad_key, grad_value)


def swap(value, axis, size, mask):
    return lax.ppermute(value, axis, [(i, i ^ mask) for i in range(size)])


def swap_both(value, reps, shards, rep_mask, shard_mask):
    pairs = []
    for r in range(reps):
        for s in range(shards):
            pairs.append((r * shards + s, (r ^ rep_mask) * shards + (s ^ shard_mask)))
    return lax.ppermute(value, ("rep", "shard"), pairs)


def shift(value, shards, steps):
    return lax.ppermute(value, "shard", [(i, (i + 2 * steps) % shards) for i in range(shards)])


def quarter(value, rep_id, reps):
    rows = value.shape[0] // reps
    return lax.dynamic_slice_in_dim(value, rep_id * rows, rows, 0)


def gather_hops(piece, reps, shards):
    rep_id = lax.axis_index("rep")
    shard_id = lax.axis_index("shard")
    z_id = shard_id // 2
    column = [piece] + [shift(piece, shards, k) for k in range(1, 4)]
    column = jnp.stack(column)
    plane = jnp.stack(
        [
            column,
            swap_both(column, reps, shards, 0, 1),
            swap_both(column, reps, shards, 2, 0),
            swap_both(column, reps, shards, 2, 1),
        ]
    )
    other = swap(plane, "rep", reps, 1)
    every = jnp.stack([plane, other])
    every = every.reshape((2, 2, 2, 4) + piece.shape)
    z_order = (z_id - jnp.arange(4)) % 4
    y_order = (shard_id % 2) ^ jnp.arange(2)
    x_order = (rep_id // 2) ^ jnp.arange(2)
    c_order = (rep_id % 2) ^ jnp.arange(2)
    every = jnp.take(every, z_order, axis=3)
    every = jnp.take(every, y_order, axis=2)
    every = jnp.take(every, x_order, axis=1)
    every = jnp.take(every, c_order, axis=0)
    every = jnp.transpose(every, (3, 2, 1, 0, 4, 5))
    return every.reshape((shards, reps) + piece.shape)


def reduce_hops(parts, reps, shards):
    rep_id = lax.axis_index("rep")
    shard_id = lax.axis_index("shard")
    z_id, y_id = shard_id // 2, shard_id % 2
    x_id, c_id = rep_id // 2, rep_id % 2
    rows, width = parts.shape[2:]
    f32 = jnp.float32
    grid = parts.reshape(4, 2, 2, 2, rows, width)
    theirs = lax.dynamic_index_in_dim(grid, 1 - c_id, 3, False)
    mine = lax.dynamic_index_in_dim(grid, c_id, 3, False)
    got = swap(theirs, "rep", reps, 1)
    total = mine.astype(f32) + got.astype(f32)
    low = total.astype(jnp.bfloat16)

    def at(value, y, x):
        value = lax.dynamic_index_in_dim(value, y, 1, False)
        return lax.dynamic_index_in_dim(value, x, 1, False)

    column = (
        at(total, y_id, x_id)
        + swap_both(at(low, 1 - y_id, x_id), reps, shards, 0, 1).astype(f32)
        + swap_both(at(low, y_id, 1 - x_id), reps, shards, 2, 0).astype(f32)
        + swap_both(at(low, 1 - y_id, 1 - x_id), reps, shards, 2, 1).astype(f32)
    )
    low = column.astype(jnp.bfloat16)
    result = lax.dynamic_index_in_dim(column, z_id, 0, False)
    for k in range(1, 4):
        part = lax.dynamic_index_in_dim(low, (z_id + k) % 4, 0, False)
        result = result + shift(part, shards, k).astype(f32)
    return result


def gather_reps(piece, reps):
    rep_id = lax.axis_index("rep")
    pair = jnp.stack([piece, swap(piece, "rep", reps, 2)])
    four = jnp.stack([pair, swap(pair, "rep", reps, 1)])
    four = jnp.take(four, (rep_id % 2) ^ jnp.arange(2), axis=0)
    four = jnp.take(four, (rep_id // 2) ^ jnp.arange(2), axis=1)
    return jnp.transpose(four, (1, 0, 2, 3)).reshape((reps,) + piece.shape)


def body(
    reps,
    shards,
    tokens,
    cotangent,
    segments,
    first_pos,
    labels,
    query_weight,
    key_weight,
    value_weight,
    out_weight,
    up_weight,
    down_weight,
    pool_weight,
    class_weight,
    query_bias,
    value_bias,
    out_bias,
    norm1_gain,
    norm1_shift,
    up_bias,
    down_bias,
    norm2_gain,
    norm2_shift,
    pool_bias,
    class_bias,
):
    rep_id = lax.axis_index("rep")
    shard_id = lax.axis_index("shard")
    model_width = tokens.shape[2]
    ff_width = up_weight.shape[1]
    blocks = ff_width // model_width
    small = (
        query_bias, value_bias, out_bias, norm1_gain, norm1_shift, up_bias, down_bias,
        norm2_gain, norm2_shift, pool_bias, class_weight.reshape(-1),
    )
    small_sizes = [item.shape[0] for item in small]
    small_row = jnp.concatenate(small)
    small_rows = -(-small_row.shape[0] // (8 * model_width)) * 8
    small_row = jnp.pad(small_row, (0, small_rows * model_width - small_row.shape[0]))
    small_row = small_row.reshape(small_rows, model_width)
    rows = query_weight.shape[0] // reps
    first = jnp.concatenate(
        [quarter(item, rep_id, reps) for item in (query_weight, key_weight, value_weight)]
        + [small_row]
    )
    fast = shards == 8 and reps == 4
    if fast:
        first_all = gather_hops(first, reps, shards)
    else:
        first_all = lax.all_gather(first, ("shard", "rep")).reshape((shards, reps) + first.shape)
    small_all = first_all[:, 0, 3 * rows :].reshape(shards, -1)
    smalls, start = [], 0
    for size in small_sizes:
        smalls.append(small_all[:, start : start + size].reshape(-1))
        start += size
    (
        query_bias_full, value_bias_full, out_bias_full, gain_one_low, shift_one_low, up_bias_full,
        down_bias_full, gain_two_low, shift_two_low, pool_bias_full, class_full,
    ) = smalls
    class_full = class_full.reshape(model_width, -1)

    def whole_rows(gathered, begin, count):
        return gathered[:, :, begin : begin + count].reshape(-1, model_width)

    query_full, key_full, value_full = [whole_rows(first_all, i * rows, rows) for i in range(3)]
    up_blocks = [up_weight[:, i * model_width : (i + 1) * model_width] for i in range(blocks)]
    second = jnp.concatenate(
        [quarter(item, rep_id, reps) for item in [out_weight] + up_blocks + [down_weight, pool_weight]]
    )
    second_all = lax.all_gather(second, ("shard", "rep")).reshape((shards, reps) + second.shape)
    out_full = whole_rows(second_all, 0, rows)
    up_full = jnp.concatenate(
        [whole_rows(second_all, (1 + i) * rows, rows) for i in range(blocks)], axis=1
    )
    down_full = whole_rows(second_all, (1 + blocks) * rows, blocks * rows)
    pool_full = whole_rows(second_all, (1 + 2 * blocks) * rows, rows)
    gain_one = gain_one_low.astype(jnp.float32)
    gain_two = gain_two_low.astype(jnp.float32)
    seq_count, length, model_width = tokens.shape
    head_count = model_width // 64
    flat_tokens = tokens.reshape(-1, model_width)
    queries = (product(flat_tokens, query_full) + query_bias_full.astype(jnp.float32)).astype(
        jnp.bfloat16
    )
    key_rows = product(flat_tokens, key_full).astype(jnp.bfloat16)
    value_rows = (product(flat_tokens, value_full) + value_bias_full.astype(jnp.float32)).astype(
        jnp.bfloat16
    )
    query_seqs = queries.reshape(seq_count, length, model_width)
    key_seqs = key_rows.reshape(seq_count, length, model_width)
    value_seqs = value_rows.reshape(seq_count, length, model_width)
    context, logsum = attention_forward(query_seqs, key_seqs, value_seqs, segments, head_count)
    context_flat = context.reshape(-1, model_width)
    attended = product(context_flat, out_full) + out_bias_full.astype(jnp.float32)
    first_sum = flat_tokens.astype(jnp.float32) + attended
    normed, normal_one, inverse_one = norm_forward(
        first_sum, gain_one, shift_one_low.astype(jnp.float32)
    )
    normed_low = normed.astype(jnp.bfloat16)
    pre_act = product(normed_low, up_full) + up_bias_full.astype(jnp.float32)
    hidden_low = jax.nn.gelu(pre_act, approximate=False).astype(jnp.bfloat16)
    ffn_out = product(hidden_low, down_full) + down_bias_full.astype(jnp.float32)
    second_sum = normed + ffn_out
    output_f, normal_two, inverse_two = norm_forward(
        second_sum, gain_two, shift_two_low.astype(jnp.float32)
    )
    output_seq = output_f.reshape(seq_count, length, model_width)
    doc_count = first_pos.shape[1]
    picker = (first_pos[:, :, None] == jnp.arange(length, dtype=jnp.int32)[None, None, :]).astype(
        jnp.float32
    )
    picked = jnp.einsum("sjl,slc->sjc", picker, output_seq, precision=highest)
    picked = picked.reshape(-1, model_width).astype(jnp.bfloat16)
    pool_pre = product(picked, pool_full) + pool_bias_full.astype(jnp.float32)
    pool_tanh = jnp.tanh(pool_pre)
    pooled_low = pool_tanh.astype(jnp.bfloat16)
    logits = product(pooled_low, class_full) + class_bias.astype(jnp.float32)
    class_count = class_bias.shape[0]
    class_peak = jnp.max(logits, axis=-1, keepdims=True)
    class_exp = jnp.exp(logits - class_peak)
    class_prob = class_exp / jnp.sum(class_exp, axis=-1, keepdims=True)
    targets = (
        labels.reshape(-1)[:, None] == jnp.arange(class_count, dtype=jnp.int32)[None, :]
    ).astype(jnp.float32)
    grad_logits = class_prob - targets
    grad_class_bias = jnp.sum(grad_logits, axis=0)
    back_query, back_key, back_value, back_out = (query_full, key_full, value_full, out_full)
    back_up, back_down, back_pool, back_class = (up_full, down_full, pool_full, class_full)
    back_gain_one, back_gain_two = (gain_one, gain_two)
    grad_class = jnp.dot(pooled_low.astype(jnp.float32).T, grad_logits, precision=highest)
    grad_pooled = jnp.dot(grad_logits, back_class.astype(jnp.float32).T, precision=highest)
    grad_pool_pre = (grad_pooled * (1.0 - pool_tanh * pool_tanh)).astype(jnp.bfloat16)
    grad_pool_bias = jnp.sum(grad_pool_pre.astype(jnp.float32), axis=0)
    grad_pool = product_left(picked, grad_pool_pre)
    grad_picked = product_right(grad_pool_pre, back_pool).reshape(seq_count, doc_count, model_width)
    grad_output = cotangent.astype(jnp.float32) + jnp.einsum(
        "sjl,sjc->slc", picker, grad_picked, precision=highest
    )
    grad_output = grad_output.reshape(-1, model_width)
    grad_second, grad_gain_two, grad_shift_two = norm_backward(
        grad_output, normal_two, inverse_two, back_gain_two
    )
    grad_ffn = grad_second.astype(jnp.bfloat16)
    grad_down_bias = jnp.sum(grad_ffn.astype(jnp.float32), axis=0)
    grad_down = product_left(hidden_low, grad_ffn)
    grad_hidden = product_right(grad_ffn, back_down)
    unused_value, gelu_back = jax.vjp(partial(jax.nn.gelu, approximate=False), pre_act)
    grad_pre = gelu_back(grad_hidden)[0].astype(jnp.bfloat16)
    grad_up_bias = jnp.sum(grad_pre.astype(jnp.float32), axis=0)
    grad_up = product_left(normed_low, grad_pre)
    grad_normed = grad_second + product_right(grad_pre, back_up)
    grad_first, grad_gain_one, grad_shift_one = norm_backward(
        grad_normed, normal_one, inverse_one, back_gain_one
    )
    grad_attended = grad_first.astype(jnp.bfloat16)
    grad_out_bias = jnp.sum(grad_attended.astype(jnp.float32), axis=0)
    grad_out = product_left(context_flat, grad_attended)
    grad_context = product_right(grad_attended, back_out).astype(jnp.bfloat16)
    grad_queries, grad_keys, grad_values = attention_backward(
        query_seqs,
        key_seqs,
        value_seqs,
        segments,
        logsum,
        grad_context.reshape(seq_count, length, model_width),
        head_count,
    )
    grad_query = product_left(flat_tokens, grad_queries)
    grad_query_bias = jnp.sum(grad_queries.astype(jnp.float32), axis=0)
    grad_key = product_left(flat_tokens, grad_keys)
    grad_value = product_left(flat_tokens, grad_values)
    grad_value_bias = jnp.sum(grad_values.astype(jnp.float32), axis=0)
    input_grad = (
        grad_first
        + product_right(grad_queries, back_query)
        + product_right(grad_keys, back_key)
        + product_right(grad_values, back_value)
    )
    valid = (segments.reshape(-1) >= 0).astype(jnp.float32)
    sums = jnp.stack(
        [
            jnp.sum(valid * jnp.sum(first_sum * first_sum, axis=-1)),
            jnp.sum(valid * jnp.sum(attended * attended, axis=-1)),
            jnp.sum(valid * jnp.sum(second_sum * second_sum, axis=-1)),
            jnp.sum(valid * jnp.sum(ffn_out * ffn_out, axis=-1)),
        ]
    )
    sums_all, valid_all, class_bias_grad = lax.psum(
        (sums, jnp.sum(valid), grad_class_bias), ("rep", "shard")
    )
    rms = jnp.sqrt(sums_all / (valid_all * model_width))
    low = jnp.bfloat16

    def by_piece(grad):
        return grad.astype(low).reshape(shards, reps, -1, model_width)

    def scatter(parts_in):
        rows_in = parts_in.shape[2]
        flat = parts_in.reshape(-1, model_width)
        return lax.psum_scatter(flat, ("shard", "rep"), scatter_dimension=0, tiled=True)

    down_part = scatter(jnp.concatenate([by_piece(grad_down), by_piece(grad_pool)], axis=2))
    up_grads = [by_piece(grad_up[:, i * model_width : (i + 1) * model_width]) for i in range(blocks)]
    up_part = scatter(jnp.concatenate(up_grads + [by_piece(grad_out)], axis=2))
    small_grads = (
        grad_query_bias, grad_value_bias, grad_out_bias, grad_gain_one, grad_shift_one,
        grad_up_bias, grad_down_bias, grad_gain_two, grad_shift_two, grad_pool_bias,
        grad_class.reshape(-1),
    )
    small_grad = jnp.concatenate([item.reshape(shards, -1) for item in small_grads], axis=1)
    small_grad = jnp.pad(
        small_grad, ((0, 0), (0, small_rows * model_width - small_grad.shape[1]))
    ).astype(low).reshape(shards, 1, small_rows, model_width)
    small_grad = jnp.broadcast_to(small_grad, (shards, reps, small_rows, model_width))
    last = jnp.concatenate(
        [by_piece(grad_query), by_piece(grad_key), by_piece(grad_value), small_grad], axis=2
    )
    if fast:
        last_part = reduce_hops(last, reps, shards)
    else:
        last_part = scatter(last).astype(jnp.float32)
    small_out = last_part[3 * rows :].reshape(-1)
    final = jnp.concatenate([last_part[: 3 * rows].astype(low), down_part, up_part])
    if fast:
        final_all = gather_reps(final, reps)
    else:
        final_all = lax.all_gather(final, "rep")
    final_all = final_all.astype(jnp.float32)

    def own_rows(begin, count):
        return final_all[:, begin : begin + count].reshape(-1, model_width)

    down_at = 3 * rows
    up_at = down_at + (blocks + 1) * rows
    summed = [own_rows(i * rows, rows) for i in range(3)]
    summed.append(own_rows(up_at + blocks * rows, rows))
    summed.append(
        jnp.concatenate([own_rows(up_at + i * rows, rows) for i in range(blocks)], axis=1)
    )
    summed.append(own_rows(down_at, blocks * rows))
    summed.append(own_rows(down_at + blocks * rows, rows))
    small_parts, start = [], 0
    for size in small_sizes:
        small_parts.append(small_out[start : start + size])
        start += size
    summed.append(small_parts[-1].reshape(class_weight.shape))
    summed.extend(small_parts[:-1])
    output = output_f.reshape(seq_count, length, model_width).astype(jnp.bfloat16)
    logits_out = logits.reshape(seq_count, doc_count, class_count)
    input_grad = input_grad.reshape(seq_count, length, model_width)
    return (
        output,
        logits_out,
        input_grad,
        summed[0],
        summed[1],
        summed[2],
        summed[3],
        summed[4],
        summed[5],
        summed[6],
        summed[7],
        summed[8],
        summed[9],
        summed[10],
        summed[11],
        summed[12],
        summed[13],
        summed[14],
        summed[15],
        summed[16],
        summed[17],
        class_bias_grad,
        rms,
    )


def solution(mesh):
    return jax.shard_map(
        partial(body, mesh.shape["rep"], mesh.shape["shard"]),
        mesh=mesh,
        in_specs=(
            P(("rep", "shard"), None, None),
            P(("rep", "shard"), None, None),
            P(("rep", "shard"), None),
            P(("rep", "shard"), None),
            P(("rep", "shard"), None),
            P("shard", None),
            P("shard", None),
            P("shard", None),
            P("shard", None),
            P("shard", None),
            P("shard", None),
            P("shard", None),
            P("shard", None),
            P("shard"),
            P("shard"),
            P("shard"),
            P("shard"),
            P("shard"),
            P("shard"),
            P("shard"),
            P("shard"),
            P("shard"),
            P("shard"),
            P(),
        ),
        out_specs=(
            P(("rep", "shard"), None, None),
            P(("rep", "shard"), None, None),
            P(("rep", "shard"), None, None),
            P("shard", None),
            P("shard", None),
            P("shard", None),
            P("shard", None),
            P("shard", None),
            P("shard", None),
            P("shard", None),
            P("shard", None),
            P("shard"),
            P("shard"),
            P("shard"),
            P("shard"),
            P("shard"),
            P("shard"),
            P("shard"),
            P("shard"),
            P("shard"),
            P("shard"),
            P(),
            P(),
        ),
        check_vma=False,
    )
```
